768 devices in a mesh: dp: 8 (over y), tensor: 96 (over z, x, core).
Axes of the slice: x: 4, y: 8, z: 12, core: 2. Of those that a mesh axis runs over, the one named last changes fastest.
Arguments:
- grad_out: bfloat16 [1536, 8192], P('dp'), may hold values from -6 to 6
- gate_act: bfloat16 [1536, 16896], P('dp', 'tensor'), may hold values from -20 to 20
- up_act: bfloat16 [1536, 16896], P('dp', 'tensor'), may hold values from -6 to 6
- w_gate: bfloat16 [16896, 8192], P('tensor'), may hold values from -0.0625 to 0.0625
- w_up: bfloat16 [16896, 8192], P('tensor'), may hold values from -0.0625 to 0.0625
- w_down: bfloat16 [16896, 8192], P('tensor'), may hold values from -0.046875 to 0.046875
Outputs:
- input_grad: bfloat16 [1536, 8192], P(('dp', 'tensor'))
- down_grad: bfloat16 [16896, 8192], P('tensor', 'dp')
The draws below stay inside these ranges and needn't reach their ends.
All inputs are finite; a program needn't handle non-finite values.
Results may differ from the reference program's by a relative error of at most 0.014.
Values may be sent and summed in bfloat16 or wider, within the bound.
No kernel may reach another device: no remote copies, remote signals or barrier semaphores. Data moves between devices by JAX's collectives and lax.ppermute only.
A program may use at most 64 MiB of HBM per device.

```python
import jax
import jax.numpy as jnp
from jax import lax

D = 8192
FF = 16896
GROUP = 192
TOKENS = 1536
N_DP = 8


def raised(entries, key, source, target, parts, factor):
    def block_of(position):
        return (jnp.arange(entries.shape[position]) // (entries.shape[position] // parts)).reshape((-1,) + (1,) * (entries.ndim - 1 - position))

    first = jax.random.permutation(key, parts)[block_of(target)]
    second = (block_of(target) + parts // 2) % parts
    return jnp.where((block_of(source) == first) | (block_of(source) == second), factor * entries, entries)


def levels(rng, dims, shards, smallest, largest):
    def one(position, blocks):
        heights = jax.random.uniform(jax.random.fold_in(jax.random.fold_in(rng, 6), position), (blocks,), jnp.float32, smallest / len(shards), largest / len(shards))
        return jnp.repeat(jnp.exp(heights), dims[position] // blocks).reshape((-1,) + (1,) * (len(dims) - position - 1))

    gain = one(*shards[0])
    for cut in shards[1:]:
        gain = gain * one(*cut)
    return gain


def normal_values(rng, shape, deviation, most, pieces=(), kind=jnp.bfloat16):
    array = deviation * jax.random.normal(rng, shape, jnp.float32)
    if pieces:
        array = array * levels(rng, shape, pieces, -0.22, 0.18)
    return jnp.clip(array, -most, most).astype(kind)


def noise_with(rng, extent, spread, most, shards, heavy, held_as=jnp.bfloat16):
    result = spread * jax.random.normal(rng, extent, jnp.float32)
    if shards:
        result = result * levels(rng, extent, shards, -0.22, 0.18)
    return jnp.clip(raised(result, jax.random.fold_in(rng, 3), *heavy), -most, most).astype(held_as)


def setup_inputs(seed: int = 0) -> dict:
    key_list = jax.random.split(jax.random.key(seed), 7)
    return {
        "grad_out": noise_with(key_list[0], (TOKENS, D), 1.0, 6.0, ((0, 8),), (0, 1, 8, 2.0)),
        "gate_act": noise_with(key_list[1], (TOKENS, FF), 1.0, 20.0, ((0, 8), (1, 96)), (1, 0, 96, 4.75)),
        "up_act": normal_values(key_list[2], (TOKENS, FF), 1.0, 6.0, ((0, 8), (1, 96))),
        "w_gate": normal_values(key_list[3], (FF, D), D ** -0.5, 0.0625, ((0, 96),)),
        "w_up": normal_values(key_list[4], (FF, D), D ** -0.5, 0.0625, ((0, 96),)),
        "w_down": normal_values(key_list[5], (FF, D), FF ** -0.5, 0.046875, ((0, 96),)),
    }


def reference(grad_out, gate_act, up_act, w_gate, w_up, w_down):
    gate = gate_act.astype(jnp.float32)
    up = up_act.astype(jnp.float32)
    sig = jax.nn.sigmoid(gate)
    silu = gate * sig
    hidden = (silu * up).astype(jnp.bfloat16)
    hidden_grad = lax.dot_general(grad_out, w_down, (((1,), (1,)), ((), ())), preferred_element_type=jnp.float32)
    gate_grad = (hidden_grad * up * sig * (1.0 + gate * (1.0 - sig))).astype(jnp.bfloat16)
    up_grad = (hidden_grad * silu).astype(jnp.bfloat16)
    input_grad = (jnp.dot(gate_grad, w_gate, preferred_element_type=jnp.float32)
                  + jnp.dot(up_grad, w_up, preferred_element_type=jnp.float32)).astype(jnp.bfloat16)
    hidden_groups = hidden.reshape(N_DP, GROUP, FF)
    grad_groups = grad_out.reshape(N_DP, GROUP, D)

    def accumulate(total, pair):
        part = lax.dot_general(pair[0], pair[1], (((0,), (0,)), ((), ())), preferred_element_type=jnp.float32)
        return total + part.astype(jnp.bfloat16).astype(jnp.float32), 0

    total, unused = lax.scan(accumulate, jnp.zeros((FF, D), jnp.float32), (hidden_groups, grad_groups))
    return input_grad, total.astype(jnp.bfloat16)
```

```python
import jax
import jax.numpy as jnp
from jax import lax
from jax.sharding import Mesh, PartitionSpec as P

NY, NZ, NX, NC = 8, 12, 4, 2
PLANE = ("z", "x", "c")


def shift(n, d):
    return [(i, (i + d) % n) for i in range(n)]


def one_hot(rows, dtype):
    n = rows.shape[0]
    cols = lax.broadcasted_iota(jnp.int32, (n, n), 1)
    return (cols == rows[:, None]).astype(dtype)


def local(grad_out, gate_act, up_act, w_gate, w_up, w_down):
    f32, bf16 = jnp.float32, jnp.bfloat16
    tokens, d = grad_out.shape
    ff = gate_act.shape[1]
    share = tokens // (NX * NC)
    cols = d // NY
    xi, ci = lax.axis_index("x"), lax.axis_index("c")

    mine = lax.dynamic_slice(grad_out, ((xi * NC + ci) * share, 0), (share, d))
    mine = mine.reshape(share, NY, cols).transpose(1, 0, 2)
    with jax.named_scope("grad_y"):
        g0 = lax.all_to_all(mine, "y", 0, 0)

    gate = gate_act.astype(f32)
    up = up_act.astype(f32)
    sig = jax.nn.sigmoid(gate)
    silu = gate * sig
    hidden = (silu * up).astype(bf16)

    i = lax.iota(jnp.int32, tokens)
    j, k, t = i // (NX * share), (i // share) % NX, i % share
    order = (((xi + k) % NX) * NC + (ci + j) % NC) * share + t
    hid = jnp.dot(one_hot(order, bf16), hidden, preferred_element_type=f32).astype(bf16)
    with jax.named_scope("hidden_y"):
        hid = lax.all_to_all(
            jnp.broadcast_to(hid[None], (NY, tokens, ff)), "y", 0, 0
        )

    hidden_grad = lax.dot_general(
        grad_out, w_down, (((1,), (1,)), ((), ())), preferred_element_type=f32
    )
    gate_grad = (hidden_grad * up * sig * (1.0 + gate * (1.0 - sig))).astype(bf16)
    up_grad = (hidden_grad * silu).astype(bf16)

    per = tokens // (NZ * NX * NC)
    j, k = i // (tokens // NC), (i // (NZ * per)) % NX
    z, r = (i // per) % NZ, i % per
    order = ((z * NX + (xi + k) % NX) * NC + (ci + j) % NC) * per + r
    pick = one_hot(order, bf16)
    gate_grad = jnp.dot(pick, gate_grad, preferred_element_type=f32).astype(bf16)
    up_grad = jnp.dot(pick, up_grad, preferred_element_type=f32).astype(bf16)
    half = tokens // NC
    theirs = jnp.dot(gate_grad[half:], w_gate, preferred_element_type=f32) + jnp.dot(
        up_grad[half:], w_up, preferred_element_type=f32
    )
    with jax.named_scope("core"):
        theirs = lax.ppermute(theirs.astype(bf16), "c", shift(NC, 1))
    ours = jnp.dot(gate_grad[:half], w_gate, preferred_element_type=f32) + jnp.dot(
        up_grad[:half], w_up, preferred_element_type=f32
    )
    blk = half // NX
    total = ours + theirs.astype(f32)
    sent = total[blk:].astype(bf16)
    own = total[:blk]
    with jax.named_scope("x"):
        got = [
            lax.ppermute(sent[(k - 1) * blk : k * blk], "x", shift(NX, k))
            for k in (1, 3, 2)
        ]
    own = own + sum(a.astype(f32) for a in got)
    with jax.named_scope("z"):
        parts = lax.all_to_all(own.astype(bf16).reshape(NZ, per, d), "z", 0, 0)
    input_grad = jnp.sum(parts.astype(f32), axis=0).astype(bf16)

    g0 = g0.reshape(NY * share, cols)
    with jax.named_scope("grad_x"):
        g = [g0] + [lax.ppermute(g0, "x", shift(NX, -k)) for k in range(1, NX)]
    g = jnp.stack(g)
    with jax.named_scope("grad_core"):
        g = jnp.stack([g, lax.ppermute(g, "c", shift(NC, 1))])
    hid = hid.reshape(NY, NC * NX, share, ff).transpose(1, 0, 2, 3)
    down_grad = lax.dot_general(
        hid.reshape(NY * tokens, ff),
        g.reshape(NY * tokens, cols),
        (((0,), (0,)), ((), ())),
        preferred_element_type=f32,
    ).astype(bf16)
    return (input_grad, down_grad)


def solution(mesh):
    mesh = Mesh(mesh.devices.reshape(NY, NZ, NX, NC), ("y",) + PLANE)
    placed = (
        P("y", None),
        P("y", PLANE),
        P("y", PLANE),
        P(PLANE, None),
        P(PLANE, None),
        P(PLANE, None),
    )
    return jax.shard_map(
        local,
        mesh=mesh,
        in_specs=placed,
        out_specs=(P(("y",) + PLANE, None), P(PLANE, "y")),
        check_vma=False,
    )
```

```python
import jax
import jax.numpy as jnp
from jax import lax
from jax.experimental import pallas as pl
from jax.experimental.pallas import tpu as pltpu
from jax.sharding import Mesh, PartitionSpec as P

NY, NZ, NX, NC = 8, 12, 4, 2
PLANE = ("z", "x", "c")
PIECES = 4
CHUNKS = 4
f32, bf16 = jnp.float32, jnp.bfloat16


def shift(n, d):
    return [(i, (i + d) % n) for i in range(n)]


def dot(a, b, over):
    return lax.dot_general(a, b, (over, ((), ())), preferred_element_type=f32)


def one_hot(order):
    n = order.shape[0]
    cols = lax.broadcasted_iota(jnp.int32, (n, n), 1)
    return jnp.where(cols == order, 1.0, 0.0).astype(bf16)


def pack_kernel(at_ref, order_ref, grad_ref, gate_ref, up_ref, out_ref):
    ny, _, width = out_ref.shape
    share = grad_ref.shape[0]
    ff = gate_ref.shape[0]
    tokens = gate_ref.shape[1]
    gate = gate_ref[...].astype(f32)
    hidden = (gate * jax.nn.sigmoid(gate) * up_ref[...].astype(f32)).astype(bf16)
    hidden = dot(one_hot(order_ref[...]), hidden, ((1,), (1,))).astype(bf16)
    hidden = jnp.concatenate([hidden, jnp.zeros((tokens, width - ff), bf16)], axis=1)
    for y in range(ny):
        for b in range(PIECES):
            start = (y * PIECES + b) * width
            out_ref[y, b * share : (b + 1) * share, :] = grad_ref[
                :, start : start + width
            ]
        out_ref[y, PIECES * share :, :] = hidden


def main_kernel(
    order_ref, gate_ref, up_ref, grad_hbm, wd_hbm, wg_hbm, wu_hbm,
    theirs_ref, ours_ref, grad, wd, w, grad_sem, wd_sem, wg_sem, wu_sem,
):
    ff, d = wd.shape
    half = ours_ref.shape[0]
    step = d // CHUNKS
    chunks = [pl.ds(i * step, step) for i in range(CHUNKS)]
    copies = []
    for i, c in enumerate(chunks):
        copies.append(
            (
                pltpu.make_async_copy(grad_hbm.at[:, c], grad.at[:, c], grad_sem.at[i]),
                pltpu.make_async_copy(wd_hbm.at[:, c], wd.at[:, c], wd_sem.at[i]),
            )
        )
    weights = []
    for i, c in enumerate(chunks):
        weights.append(
            (
                pltpu.make_async_copy(wg_hbm.at[:, c], w.at[:ff, c], wg_sem.at[i]),
                pltpu.make_async_copy(wu_hbm.at[:, c], w.at[ff:, c], wu_sem.at[i]),
            )
        )
    for pair in copies + weights:
        for copy in pair:
            copy.start()

    gate = gate_ref[...].astype(f32)
    up = up_ref[...].astype(f32)
    sig = jax.nn.sigmoid(gate)
    silu = gate * sig
    slope = up * sig * (1.0 + gate * (1.0 - sig))
    pick = one_hot(order_ref[...])

    hidden_grad = jnp.zeros(gate.shape, f32)
    for pair, c in zip(copies, chunks):
        for copy in pair:
            copy.wait()
        hidden_grad = hidden_grad + dot(wd[:, c], grad[:, c], ((1,), (1,)))
    both = jnp.concatenate(
        [(hidden_grad * slope).astype(bf16), (hidden_grad * silu).astype(bf16)], axis=0
    )
    both = dot(pick, both, ((1,), (1,))).astype(bf16)
    for i, pair in enumerate(weights):
        for copy in pair:
            copy.wait()

        def body(n, carry, i=i):
            at = pl.ds(pl.multiple_of(i * step + n * 512, 512), 512)
            part = dot(both, w[:, at], ((1,), (0,))).astype(bf16)
            ours_ref[:, at] = part[:half]
            theirs_ref[:, at] = part[half:]
            return carry

        lax.fori_loop(0, step // 512, body, 0)


def down_kernel(own_ref, x1_ref, x2_ref, x3_ref, core_ref, out_ref, h, g):
    ny, _, width = own_ref.shape
    ff = out_ref.shape[0]
    share = x1_ref.shape[1] // PIECES
    block = ny * share
    for j in range(NC):
        for k in range(NX):
            jk = j * NX + k
            at = PIECES * share + jk * share
            h[jk * block : (jk + 1) * block, :] = own_ref[:, at : at + share, :].reshape(
                block, width
            )
            for b in range(PIECES):
                rows_b = slice(b * share, (b + 1) * share)
                if j == 1:
                    piece = core_ref[k, :, rows_b, :]
                else:
                    piece = (own_ref, x1_ref, x2_ref, x3_ref)[k][:, rows_b, :]
                g[jk * block : (jk + 1) * block, b * width : (b + 1) * width] = (
                    piece.reshape(block, width)
                )
    left = h[...]
    for b in range(PIECES):
        c = slice(b * width, (b + 1) * width)
        out_ref[:, c] = dot(left, g[:, c], ((0,), (0,)))[:ff].astype(bf16)


VMEM = pl.BlockSpec(memory_space=pltpu.VMEM)
ANY = pl.BlockSpec(memory_space=pl.ANY)


def local(grad_out, gate_act, up_act, w_gate, w_up, w_down):
    tokens, d = grad_out.shape
    ff = gate_act.shape[1]
    share = tokens // (NX * NC)
    cols = d // NY
    width = cols // PIECES
    per = tokens // (NZ * NX * NC)
    half = tokens // NC
    xi, ci = lax.axis_index("x"), lax.axis_index("c")
    gate_t, up_t = gate_act.T, up_act.T

    i = lax.iota(jnp.int32, tokens)
    j, k, t = i // (NX * share), (i // share) % NX, i % share
    by_share = (((xi + k) % NX) * NC + (ci + j) % NC) * share + t
    k, z, r = (i // (NZ * per)) % NX, (i // per) % NZ, i % per
    j = i // half
    by_owner = ((z * NX + (xi + k) % NX) * NC + (ci + j) % NC) * per + r

    packed = pl.pallas_call(
        pack_kernel,
        name="pack",
        grid_spec=pltpu.PrefetchScalarGridSpec(
            num_scalar_prefetch=1,
            grid=(1,),
            in_specs=[
                pl.BlockSpec((tokens, 1), lambda g, at: (0, 0)),
                pl.BlockSpec((share, d), lambda g, at: (at[0], 0)),
                pl.BlockSpec((ff, tokens), lambda g, at: (0, 0)),
                pl.BlockSpec((ff, tokens), lambda g, at: (0, 0)),
            ],
            out_specs=pl.BlockSpec(
                (NY, PIECES * share + tokens, width), lambda g, at: (0, 0, 0)
            ),
        ),
        out_shape=jax.ShapeDtypeStruct((NY, PIECES * share + tokens, width), bf16),
        cost_estimate=pl.CostEstimate(
            flops=2 * tokens * tokens * ff, bytes_accessed=2_000_000, transcendentals=0
        ),
    )((xi * NC + ci)[None], by_share[:, None], grad_out, gate_t, up_t)
    packed = lax.all_to_all(packed, "y", 0, 0)

    theirs, ours = pl.pallas_call(
        main_kernel,
        name="main",
        in_specs=[VMEM, VMEM, VMEM, ANY, ANY, ANY, ANY],
        out_specs=[VMEM, VMEM],
        out_shape=[jax.ShapeDtypeStruct((half, d), bf16)] * 2,
        scratch_shapes=[
            pltpu.VMEM((tokens, d), bf16),
            pltpu.VMEM((ff, d), bf16),
            pltpu.VMEM((2 * ff, d), bf16),
        ]
        + [pltpu.SemaphoreType.DMA((CHUNKS,))] * 4,
        cost_estimate=pl.CostEstimate(
            flops=6 * tokens * ff * d, bytes_accessed=14_000_000, transcendentals=0
        ),
    )(by_owner[:, None], gate_t, up_t, grad_out, w_down, w_gate, w_up)
    theirs = lax.ppermute(theirs, "c", shift(NC, 1))
    total = ours.astype(f32) + theirs.astype(f32)
    blk = half // NX
    own = total[:blk]
    sent = total[blk:].astype(bf16)
    got = [
        lax.ppermute(sent[(k - 1) * blk : k * blk], "x", shift(NX, k))
        for k in (1, 3, 2)
    ]
    own = own + sum(a.astype(f32) for a in got)
    parts = lax.all_to_all(own.astype(bf16).reshape(NZ, per, d), "z", 0, 0)
    input_grad = jnp.sum(parts.astype(f32), axis=0).astype(bf16)

    g0 = packed[:, : PIECES * share, :]
    g = [lax.ppermute(g0, "x", shift(NX, -k)) for k in range(1, NX)]
    other = lax.ppermute(jnp.stack([g0] + g), "c", shift(NC, 1))
    down_grad = pl.pallas_call(
        down_kernel,
        name="down",
        in_specs=[VMEM] * 5,
        out_specs=VMEM,
        out_shape=jax.ShapeDtypeStruct((ff, cols), bf16),
        scratch_shapes=[
            pltpu.VMEM((NY * tokens, width), bf16),
            pltpu.VMEM((NY * tokens, cols), bf16),
        ],
        cost_estimate=pl.CostEstimate(
            flops=2 * NY * tokens * ff * cols, bytes_accessed=8_000_000, transcendentals=0
        ),
    )(packed, *g, other)
    return (input_grad, down_grad)


def solution(mesh):
    mesh4 = Mesh(mesh.devices.reshape(NY, NZ, NX, NC), ("y",) + PLANE)
    placed = (
        P("y", None),
        P("y", PLANE),
        P("y", PLANE),
        P(PLANE, None),
        P(PLANE, None),
        P(PLANE, None),
    )
    return jax.shard_map(
        local,
        mesh=mesh4,
        in_specs=placed,
        out_specs=(P(("y",) + PLANE, None), P(PLANE, "y")),
        check_vma=False,
    )
```

```python
import jax
import jax.numpy as jnp
import numpy as np
from jax import lax
from jax.experimental import pallas as pl
from jax.experimental.pallas import tpu as pltpu
from jax.sharding import Mesh, PartitionSpec as P

NY, NZ, NX, NC = 8, 12, 4, 2
PLANE = ("z", "x", "c")
CHUNKS = 4
PIECES = 4
LANES = 128
f32, bf16 = jnp.float32, jnp.bfloat16


VMEM = pl.BlockSpec(memory_space=pltpu.VMEM)
HBM = pl.BlockSpec(memory_space=pltpu.HBM)


def shift(n, d):
    return [(i, (i + d) % n) for i in range(n)]


def round_x(step):
    return [
        (x * NC + c, (x + step * (1 - 2 * c)) % NX * NC + c)
        for x in range(NX)
        for c in range(NC)
    ]


def dot(a, b, over):
    return lax.dot_general(a, b, (over, ((), ())), preferred_element_type=f32)


def one_hot(order):
    n = order.shape[0]
    cols = lax.broadcasted_iota(jnp.int32, (n, n), 1)
    return jnp.where(cols == order, 1.0, 0.0).astype(bf16)


def tables(tokens):
    share = tokens // (NX * NC)
    per = share // NZ
    i = np.arange(tokens)
    j, k, rest = i // (NX * share), (i // share) % NX, i % share
    by_owner = (rest // per) * (NX * NC * per) + rest % per
    return np.stack([k, j, rest, by_owner], axis=1).astype(np.int32)


def rows_of(table, base, x_step, c_step):
    c = (lax.axis_index("c") + table[:, 1:2]) & (NC - 1)
    x = (lax.axis_index("x") + table[:, 0:1] * (1 - 2 * c)) & (NX - 1)
    return table[:, base : base + 1] + x * x_step + c * c_step


def pack_kernel(
    table_hbm, gate_hbm, up_hbm, grad_hbm, packed_hbm,
    table, gate_v, up_v, grad, mine, hid, small_sem, grad_sem, mine_sem, hid_sem,
):
    ff, tokens = gate_v.shape
    ny, mine_rows, width = mine.shape
    share = grad.shape[1]
    small = [
        pltpu.make_async_copy(a, b, small_sem.at[i])
        for i, (a, b) in enumerate(
            ((gate_hbm, gate_v), (up_hbm, up_v), (table_hbm, table))
        )
    ]
    x, c = lax.axis_index("x"), lax.axis_index("c")
    for n in range(2):
        first = (((x + 2 * n) & (NX - 1)) * NC + c) * share
        rows = pl.ds(pl.multiple_of(first, 8), share)
        small.append(
            pltpu.make_async_copy(grad_hbm.at[rows, :], grad.at[n], grad_sem.at[n])
        )
    for copy in small:
        copy.start()
    for copy in small[:3]:
        copy.wait()
    gate = gate_v[...].astype(f32)
    hidden = (gate * jax.nn.sigmoid(gate) * up_v[...].astype(f32)).astype(bf16)
    order = rows_of(table[...], 2, NC * share, share)
    hidden = dot(one_hot(order), hidden, ((1,), (1,))).astype(bf16)
    half, quarter = tokens // 2, tokens // 4
    for n in range(2):
        lanes = slice(n * LANES, (n + 1) * LANES)
        hid[:half, lanes] = hidden[n * half : (n + 1) * half, :LANES]
    rest = jnp.zeros((quarter, LANES // 2 - (ff - LANES)), bf16)
    for n in range(2):
        lanes = slice(n * LANES, (n + 1) * LANES)
        groups = []
        for m in (2 * n, 2 * n + 1):
            groups += [hidden[m * quarter : (m + 1) * quarter, LANES:], rest]
        hid[half:, lanes] = jnp.concatenate(groups, axis=1)
    stores = [
        pltpu.make_async_copy(hid, packed_hbm.at[y, mine_rows:, :], hid_sem.at[y])
        for y in range(ny)
    ]
    for copy in stores:
        copy.start()
    for copy in small[3:]:
        copy.wait()
    for y in range(ny):
        for n in range(2):
            for b in range(PIECES):
                start = (y * PIECES + b) * width
                row = (n * PIECES + b) * share
                mine[y, row : row + share, :] = grad[n, :, start : start + width]
        copy = pltpu.make_async_copy(
            mine.at[y], packed_hbm.at[y, :mine_rows, :], mine_sem.at[y]
        )
        copy.start()
        stores.append(copy)
    for copy in stores:
        copy.wait()


def main_kernel(
    table_hbm, gate_hbm, up_hbm, grad_hbm, wd_hbm, wg_hbm, wu_hbm,
    their_far, their_near, our_far, our_near,
    table, gate_v, up_v, grad, wd, w, small_sem, grad_sem, wd_sem, wg_sem, wu_sem,
):
    _, d = grad.shape
    ff = wd.shape[0]
    blk = our_far.shape[0]
    step = d // CHUNKS
    chunks = [pl.ds(i * step, step) for i in range(CHUNKS)]
    small = [
        pltpu.make_async_copy(a, b, small_sem.at[i])
        for i, (a, b) in enumerate(
            ((gate_hbm, gate_v), (up_hbm, up_v), (table_hbm, table))
        )
    ]
    loads = [
        (
            pltpu.make_async_copy(grad_hbm.at[:, c], grad.at[:, c], grad_sem.at[i]),
            pltpu.make_async_copy(wd_hbm.at[:, c], wd.at[:, c], wd_sem.at[i]),
        )
        for i, c in enumerate(chunks)
    ]
    weights = [
        (
            pltpu.make_async_copy(wg_hbm.at[:, c], w.at[:ff, c], wg_sem.at[i]),
            pltpu.make_async_copy(wu_hbm.at[:, c], w.at[ff:, c], wu_sem.at[i]),
        )
        for i, c in enumerate(chunks)
    ]
    for copy in small:
        copy.start()
    for pair in loads + weights:
        for copy in pair:
            copy.start()

    for copy in small:
        copy.wait()
    gate = gate_v[...].astype(f32)
    up = up_v[...].astype(f32)
    sig = jax.nn.sigmoid(gate)
    silu = gate * sig
    slope = up * sig * (1.0 + gate * (1.0 - sig))
    per = blk // NZ
    pick = one_hot(rows_of(table[...], 3, NC * per, per))
    hidden_grad = jnp.zeros(gate.shape, f32)
    for pair, c in zip(loads, chunks):
        for copy in pair:
            copy.wait()
        hidden_grad = hidden_grad + dot(wd[:, c], grad[:, c], ((1,), (1,)))
    both = jnp.concatenate(
        [(hidden_grad * slope).astype(bf16), (hidden_grad * silu).astype(bf16)], axis=0
    )
    both = dot(pick, both, ((1,), (1,))).astype(bf16)
    for i, pair in enumerate(weights):
        for copy in pair:
            copy.wait()
        for n in range(step // 512):
            at = slice(i * step + n * 512, i * step + (n + 1) * 512)
            part = dot(both, w[:, at], ((1,), (0,))).astype(bf16)
            for far, near, first in (
                (our_far, our_near, 0),
                (their_far, their_near, NX),
            ):
                rows = [
                    part[(first + k) * blk : (first + k + 1) * blk] for k in range(NX)
                ]
                near[:blk, at] = rows[0]
                near[blk : 2 * blk, at] = rows[1]
                far[:, at] = rows[2]
                near[2 * blk :, at] = rows[3]


def add_kernel(a_ref, b_ref, out_ref):
    out_ref[...] = (a_ref[...].astype(f32) + b_ref[...].astype(f32)).astype(bf16)


def near_kernel(a_ref, b_ref, own_ref, via_ref, other_ref):
    blk = own_ref.shape[0]
    for n, ref in enumerate((own_ref, via_ref, other_ref)):
        rows = slice(n * blk, (n + 1) * blk)
        total = a_ref[rows].astype(f32) + b_ref[rows].astype(f32)
        ref[...] = total.astype(ref.dtype)


def own_kernel(own_ref, via_ref, other_ref, out_ref):
    nz, per, _ = out_ref.shape
    total = own_ref[...] + via_ref[...].astype(f32) + other_ref[...].astype(f32)
    for z in range(nz):
        out_ref[z] = total[z * per : (z + 1) * per].astype(bf16)


def total_kernel(parts_ref, out_ref):
    total = parts_ref[0].astype(f32)
    for z in range(1, parts_ref.shape[0]):
        total = total + parts_ref[z].astype(f32)
    out_ref[...] = total.astype(bf16)


def gather_rows(jks, piece_of, own_ref, h, g):
    ny, _, width = own_ref.shape
    block = h.shape[0] // len(jks)
    share = block // ny
    for n, jk in enumerate(jks):
        rows = slice(n * block, (n + 1) * block)
        first = 2 * PIECES * share
        at, lane = first + jk % 4 * share, jk // 4 * LANES
        h[rows, :LANES] = own_ref[:, at : at + share, lane : lane + LANES].reshape(
            block, LANES
        )
        at, lane = first + (4 + jk % 2) * share, jk // 2 * (LANES // 2)
        h[rows, LANES:] = own_ref[
            :, at : at + share, lane : lane + h.shape[1] - LANES
        ].reshape(block, h.shape[1] - LANES)
        for b in range(PIECES):
            piece = piece_of(jk, b, share)
            g[rows, b * width : (b + 1) * width] = piece.reshape(block, width)


def down_kernel(own_ref, side_ref, core_ref, out_ref, h, g):
    def piece_of(jk, b, share):
        first = (jk % NX // 2 * PIECES + b) * share
        ref = side_ref if jk % 2 else (own_ref if jk < NX else core_ref)
        return ref[:, first : first + share, :]

    gather_rows((0, 1, 2, 3, NX, NX + 2), piece_of, own_ref, h, g)
    left = h[...]
    width = own_ref.shape[2]
    for b in range(PIECES):
        c = slice(b * width, (b + 1) * width)
        out_ref[:, c] = dot(left, g[:, c], ((0,), (0,)))


def last_kernel(own_ref, side_ref, sum_ref, out_ref, h, g):
    def piece_of(jk, b, share):
        first = (jk % NX // 2 * PIECES + b) * share
        return side_ref[:, first : first + share, :]

    gather_rows((NX + 1, NX + 3), piece_of, own_ref, h, g)
    left = h[...]
    width = own_ref.shape[2]
    for b in range(PIECES):
        c = slice(b * width, (b + 1) * width)
        part = dot(left, g[:, c], ((0,), (0,)))
        out_ref[:, c] = (sum_ref[:, c] + part).astype(bf16)


def call(kernel, specs, outs, flops, nbytes, scratch=(), in_hbm=(), auto=False, mib=16, dtype=None):
    dtypes = dtype or (bf16,) * len(outs)
    run = pl.pallas_call(
        kernel,
        in_specs=specs,
        out_specs=[HBM if n in in_hbm else VMEM for n in range(len(outs))],
        out_shape=[
            jax.ShapeDtypeStruct(s, t) if auto or n in in_hbm else pltpu.VMEM(s, t)
            for n, (s, t) in enumerate(zip(outs, dtypes))
        ],
        scratch_shapes=list(scratch),
        compiler_params=pltpu.CompilerParams(vmem_limit_bytes=mib << 20),
        cost_estimate=pl.CostEstimate(
            flops=flops, bytes_accessed=nbytes, transcendentals=0
        ),
    )

    def on_chip(*args):
        made = run(
            *(
                pltpu.with_memory_space_constraint(a, pltpu.VMEM) if s is VMEM else a
                for a, s in zip(args, specs)
            )
        )
        return [
            o if auto or n in in_hbm else pltpu.with_memory_space_constraint(o, pltpu.VMEM)
            for n, o in enumerate(made)
        ]

    return on_chip


def local(grad_out, gate_act, up_act, w_gate, w_up, w_down):
    tokens, d = grad_out.shape
    ff = gate_act.shape[1]
    share = tokens // (NX * NC)
    cols = d // NY
    width = cols // PIECES
    blk = tokens // NC // NX
    table = jnp.asarray(tables(tokens))
    gate_t, up_t = gate_act.T, up_act.T

    packed_rows = 2 * PIECES * share + tokens // 2 + tokens // 4
    dma = pltpu.SemaphoreType.DMA
    small = [
        pltpu.VMEM(table.shape, jnp.int32),
        pltpu.VMEM((ff, tokens), bf16),
        pltpu.VMEM((ff, tokens), bf16),
    ]
    (packed,) = call(
        pack_kernel,
        [HBM] * 4,
        [(NY, packed_rows, width)],
        2 * tokens * tokens * ff,
        4_000_000,
        small
        + [
            pltpu.VMEM((2, share, d), bf16),
            pltpu.VMEM((NY, 2 * PIECES * share, width), bf16),
            pltpu.VMEM((packed_rows - 2 * PIECES * share, width), bf16),
            dma((3,)),
            dma((2,)),
            dma((NY,)),
            dma((NY,)),
        ],
        in_hbm=(0,),
        mib=63,
    )(table, gate_t, up_t, grad_out)
    packed = lax.all_to_all(packed, "y", 0, 0)

    their_far, their_near, our_far, our_near = call(
        main_kernel,
        [HBM] * 7,
        [(blk, d), (3 * blk, d), (blk, d), (3 * blk, d)],
        6 * tokens * ff * d,
        15_000_000,
        small
        + [
            pltpu.VMEM((tokens, d), bf16),
            pltpu.VMEM((ff, d), bf16),
            pltpu.VMEM((2 * ff, d), bf16),
            dma((3,)),
        ]
        + [dma((CHUNKS,))] * 4,
        mib=58,
    )(table, gate_t, up_t, grad_out, w_down, w_gate, w_up)
    their_far = lax.ppermute(their_far, "c", shift(NC, 1))
    their_near = lax.ppermute(their_near, "c", shift(NC, 1))
    (far,) = call(add_kernel, [VMEM] * 2, [(blk, d)], blk * d, 6 * blk * d)(
        our_far, their_far
    )
    far = lax.ppermute(far, ("x", "c"), round_x(1))
    own, via, other = call(
        near_kernel,
        [VMEM] * 2,
        [(blk, d)] * 3,
        3 * blk * d,
        22 * blk * d,
        dtype=(f32, f32, bf16),
    )(our_near, their_near)
    other = lax.ppermute(other, ("x", "c"), round_x(-1))
    (via,) = call(add_kernel, [VMEM] * 2, [(blk, d)], blk * d, 8 * blk * d)(via, far)
    via = lax.ppermute(via, ("x", "c"), round_x(1))
    (own,) = call(
        own_kernel, [VMEM] * 3, [(NZ, blk // NZ, d)], 2 * blk * d, 10 * blk * d
    )(own, via, other)
    parts = lax.all_to_all(own, "z", 0, 0)
    (input_grad,) = call(
        total_kernel, [VMEM], [(blk // NZ, d)], blk * d, 3 * blk * d, auto=True
    )(parts)

    mine = packed[:, : 2 * PIECES * share, :]
    side = lax.ppermute(mine, ("x", "c"), round_x(-1))
    core = lax.ppermute(mine, "c", shift(NC, 1))
    side_core = lax.ppermute(side, "c", shift(NC, 1))
    early, late = 6 * NY * share, 2 * NY * share
    (part,) = call(
        down_kernel,
        [VMEM] * 3,
        [(ff, cols)],
        2 * early * ff * cols,
        6_000_000,
        [pltpu.VMEM((early, ff), bf16), pltpu.VMEM((early, cols), bf16)],
        dtype=(f32,),
    )(packed, side, core)
    (down_grad,) = call(
        last_kernel,
        [VMEM] * 3,
        [(ff, cols)],
        2 * late * ff * cols,
        3_000_000,
        [pltpu.VMEM((late, ff), bf16), pltpu.VMEM((late, cols), bf16)],
        auto=True,
    )(packed, side_core, part)
    return (input_grad, down_grad)


def solution(mesh):
    mesh4 = Mesh(mesh.devices.reshape(NY, NZ, NX, NC), ("y",) + PLANE)
    placed = (
        P("y", None),
        P("y", PLANE),
        P("y", PLANE),
        P(PLANE, None),
        P(PLANE, None),
        P(PLANE, None),
    )
    return jax.shard_map(
        local,
        mesh=mesh4,
        in_specs=placed,
        out_specs=(P(("y",) + PLANE, None), P(PLANE, "y")),
        check_vma=False,
    )
```

```python
import jax
import jax.numpy as jnp
import numpy as np
from jax import lax
from jax.experimental import pallas as pl
from jax.experimental.pallas import tpu as pltpu
from jax.sharding import Mesh, PartitionSpec as P

NY, NZ, NX, NC = 8, 12, 4, 2
PLANE = ("z", "x", "c")
CHUNKS = 4
HEAD = 2
PIECES = 4
LANES = 128
f32, bf16 = jnp.float32, jnp.bfloat16


VMEM = pl.BlockSpec(memory_space=pltpu.VMEM)
HBM = pl.BlockSpec(memory_space=pltpu.HBM)


def shift(n, d):
    return [(i, (i + d) % n) for i in range(n)]


def round_x(step):
    return [
        (x * NC + c, (x + step * (1 - 2 * c)) % NX * NC + c)
        for x in range(NX)
        for c in range(NC)
    ]


def dot(a, b, over):
    return lax.dot_general(a, b, (over, ((), ())), preferred_element_type=f32)


def one_hot(order):
    n = order.shape[0]
    cols = lax.broadcasted_iota(jnp.int32, (n, n), 1)
    return jnp.where(cols == order, 1.0, 0.0).astype(bf16)


def tables(tokens):
    share = tokens // (NX * NC)
    per = share // NZ
    i = np.arange(tokens)
    j, k, rest = i // (NX * share), (i // share) % NX, i % share
    by_owner = (rest // per) * (NX * NC * per) + rest % per
    return np.stack([k, j, rest, by_owner], axis=1).astype(np.int32)


def rows_of(table, base, x_step, c_step):
    c = (lax.axis_index("c") + table[:, 1:2]) & (NC - 1)
    x = (lax.axis_index("x") + table[:, 0:1] * (1 - 2 * c)) & (NX - 1)
    return table[:, base : base + 1] + x * x_step + c * c_step


def load_chunks(grad_hbm, wd_hbm, grad, wd, grad_sem, wd_sem, first):
    step = grad_hbm.shape[1] // CHUNKS
    pairs = []
    for i in range(grad.shape[1] // step):
        here, there = pl.ds((first + i) * step, step), pl.ds(i * step, step)
        pairs.append(
            (
                pltpu.make_async_copy(
                    grad_hbm.at[:, here], grad.at[:, there], grad_sem.at[i]
                ),
                pltpu.make_async_copy(wd_hbm.at[:, here], wd.at[:, there], wd_sem.at[i]),
            )
        )
    return pairs


def contract(loads, grad, wd, behind=()):
    step = grad.shape[1] // len(loads)
    total = jnp.zeros((wd.shape[0], grad.shape[0]), f32)
    for i, pair in enumerate(loads):
        for copy in pair:
            copy.wait()
        for copy in behind[i * len(behind) // len(loads) :][: len(behind) // len(loads)]:
            copy.start()
        at = slice(i * step, (i + 1) * step)
        total = total + dot(wd[:, at], grad[:, at], ((1,), (1,)))
    return total


def pack_kernel(
    table_hbm, gate_hbm, up_hbm, grad_hbm, wd_hbm, packed_hbm, part_ref,
    table, gate_v, up_v, grad, mine, hid, gradc, wd,
    small_sem, grad_sem, mine_sem, hid_sem, gradc_sem, wd_sem,
):
    ff, tokens = gate_v.shape
    ny, mine_rows, width = mine.shape
    share = grad.shape[1]
    small = [
        pltpu.make_async_copy(a, b, small_sem.at[i])
        for i, (a, b) in enumerate(
            ((gate_hbm, gate_v), (up_hbm, up_v), (table_hbm, table))
        )
    ]
    x, c = lax.axis_index("x"), lax.axis_index("c")
    for n in range(2):
        first = (((x + 2 * n) & (NX - 1)) * NC + c) * share
        rows = pl.ds(pl.multiple_of(first, 8), share)
        small.append(
            pltpu.make_async_copy(grad_hbm.at[rows, :], grad.at[n], grad_sem.at[n])
        )
    loads = load_chunks(grad_hbm, wd_hbm, gradc, wd, gradc_sem, wd_sem, 0)
    for copy in small:
        copy.start()
    for pair in loads:
        for copy in pair:
            copy.start()
    for copy in small[:3]:
        copy.wait()
    gate = gate_v[...].astype(f32)
    hidden = (gate * jax.nn.sigmoid(gate) * up_v[...].astype(f32)).astype(bf16)
    order = rows_of(table[...], 2, NC * share, share)
    hidden = dot(one_hot(order), hidden, ((1,), (1,))).astype(bf16)
    half, quarter = tokens // 2, tokens // 4
    for n in range(2):
        lanes = slice(n * LANES, (n + 1) * LANES)
        hid[:half, lanes] = hidden[n * half : (n + 1) * half, :LANES]
    rest = jnp.zeros((quarter, LANES // 2 - (ff - LANES)), bf16)
    for n in range(2):
        lanes = slice(n * LANES, (n + 1) * LANES)
        groups = []
        for m in (2 * n, 2 * n + 1):
            groups += [hidden[m * quarter : (m + 1) * quarter, LANES:], rest]
        hid[half:, lanes] = jnp.concatenate(groups, axis=1)
    stores = [
        pltpu.make_async_copy(hid, packed_hbm.at[y, mine_rows:, :], hid_sem.at[y])
        for y in range(ny)
    ]
    for copy in stores:
        copy.start()
    for copy in small[3:]:
        copy.wait()
    for y in range(ny):
        for n in range(2):
            for b in range(PIECES):
                start = (y * PIECES + b) * width
                row = (n * PIECES + b) * share
                mine[y, row : row + share, :] = grad[n, :, start : start + width]
        copy = pltpu.make_async_copy(
            mine.at[y], packed_hbm.at[y, :mine_rows, :], mine_sem.at[y]
        )
        copy.start()
        stores.append(copy)
    part_ref[...] = contract(loads, gradc, wd)
    for copy in stores:
        copy.wait()


def main_kernel(
    part_ref, table_hbm, gate_hbm, up_hbm, grad_hbm, wd_hbm, wg_hbm, wu_hbm,
    their_far, their_near, our_far, our_near,
    table, gate_v, up_v, grad, wd, w, small_sem, grad_sem, wd_sem, wg_sem, wu_sem,
):
    d = w.shape[1]
    ff = wd.shape[0]
    blk = our_far.shape[0]
    step = d // CHUNKS
    chunks = [pl.ds(i * step, step) for i in range(CHUNKS)]
    small = [
        pltpu.make_async_copy(a, b, small_sem.at[i])
        for i, (a, b) in enumerate(
            ((gate_hbm, gate_v), (up_hbm, up_v), (table_hbm, table))
        )
    ]
    loads = load_chunks(grad_hbm, wd_hbm, grad, wd, grad_sem, wd_sem, HEAD)
    weights = [
        (
            pltpu.make_async_copy(wg_hbm.at[:, c], w.at[:ff, c], wg_sem.at[i]),
            pltpu.make_async_copy(wu_hbm.at[:, c], w.at[ff:, c], wu_sem.at[i]),
        )
        for i, c in enumerate(chunks)
    ]
    for copy in small:
        copy.start()
    for pair in loads:
        for copy in pair:
            copy.start()

    for copy in small:
        copy.wait()
    gate = gate_v[...].astype(f32)
    up = up_v[...].astype(f32)
    sig = jax.nn.sigmoid(gate)
    silu = gate * sig
    slope = up * sig * (1.0 + gate * (1.0 - sig))
    per = blk // NZ
    pick = one_hot(rows_of(table[...], 3, NC * per, per))
    behind = [copy for pair in weights for copy in pair]
    hidden_grad = part_ref[...] + contract(loads, grad, wd, behind)
    both = jnp.concatenate(
        [(hidden_grad * slope).astype(bf16), (hidden_grad * silu).astype(bf16)], axis=0
    )
    both = dot(pick, both, ((1,), (1,))).astype(bf16)
    for i, pair in enumerate(weights):
        for copy in pair:
            copy.wait()
        for n in range(step // 512):
            at = slice(i * step + n * 512, i * step + (n + 1) * 512)
            part = dot(both, w[:, at], ((1,), (0,))).astype(bf16)
            for far, near, first in (
                (our_far, our_near, 0),
                (their_far, their_near, NX),
            ):
                rows = [
                    part[(first + k) * blk : (first + k + 1) * blk] for k in range(NX)
                ]
                near[:blk, at] = rows[0]
                near[blk : 2 * blk, at] = rows[1]
                far[:, at] = rows[2]
                near[2 * blk :, at] = rows[3]


def add_kernel(a_ref, b_ref, out_ref):
    out_ref[...] = (a_ref[...].astype(f32) + b_ref[...].astype(f32)).astype(bf16)


def near_kernel(a_ref, b_ref, own_ref, via_ref, other_ref):
    blk = own_ref.shape[0]
    for n, ref in enumerate((own_ref, via_ref, other_ref)):
        rows = slice(n * blk, (n + 1) * blk)
        total = a_ref[rows].astype(f32) + b_ref[rows].astype(f32)
        ref[...] = total.astype(ref.dtype)


def own_kernel(own_ref, via_ref, other_ref, out_ref):
    nz, per, _ = out_ref.shape
    total = own_ref[...] + via_ref[...].astype(f32) + other_ref[...].astype(f32)
    for z in range(nz):
        out_ref[z] = total[z * per : (z + 1) * per].astype(bf16)


def total_kernel(parts_ref, out_ref):
    total = parts_ref[0].astype(f32)
    for z in range(1, parts_ref.shape[0]):
        total = total + parts_ref[z].astype(f32)
    out_ref[...] = total.astype(bf16)


def gather_rows(jks, piece_of, own_ref, h, g):
    ny, _, width = own_ref.shape
    block = h.shape[0] // len(jks)
    share = block // ny
    for n, jk in enumerate(jks):
        rows = slice(n * block, (n + 1) * block)
        first = 2 * PIECES * share
        at, lane = first + jk % 4 * share, jk // 4 * LANES
        h[rows, :LANES] = own_ref[:, at : at + share, lane : lane + LANES].reshape(
            block, LANES
        )
        at, lane = first + (4 + jk % 2) * share, jk // 2 * (LANES // 2)
        h[rows, LANES:] = own_ref[
            :, at : at + share, lane : lane + h.shape[1] - LANES
        ].reshape(block, h.shape[1] - LANES)
        for b in range(PIECES):
            piece = piece_of(jk, b, share)
            g[rows, b * width : (b + 1) * width] = piece.reshape(block, width)


def down_kernel(own_ref, side_ref, core_ref, out_ref, h, g):
    def piece_of(jk, b, share):
        first = (jk % NX // 2 * PIECES + b) * share
        ref = side_ref if jk % 2 else (own_ref if jk < NX else core_ref)
        return ref[:, first : first + share, :]

    gather_rows((0, 1, 2, 3, NX, NX + 2), piece_of, own_ref, h, g)
    left = h[...]
    width = own_ref.shape[2]
    for b in range(PIECES):
        c = slice(b * width, (b + 1) * width)
        out_ref[:, c] = dot(left, g[:, c], ((0,), (0,)))


def last_kernel(own_ref, side_ref, sum_ref, out_ref, h, g):
    def piece_of(jk, b, share):
        first = (jk % NX // 2 * PIECES + b) * share
        return side_ref[:, first : first + share, :]

    gather_rows((NX + 1, NX + 3), piece_of, own_ref, h, g)
    left = h[...]
    width = own_ref.shape[2]
    for b in range(PIECES):
        c = slice(b * width, (b + 1) * width)
        part = dot(left, g[:, c], ((0,), (0,)))
        out_ref[:, c] = (sum_ref[:, c] + part).astype(bf16)


def call(kernel, specs, outs, flops, nbytes, scratch=(), in_hbm=(), auto=False, mib=16, dtype=None):
    dtypes = dtype or (bf16,) * len(outs)
    run = pl.pallas_call(
        kernel,
        in_specs=specs,
        out_specs=[HBM if n in in_hbm else VMEM for n in range(len(outs))],
        out_shape=[
            jax.ShapeDtypeStruct(s, t) if auto or n in in_hbm else pltpu.VMEM(s, t)
            for n, (s, t) in enumerate(zip(outs, dtypes))
        ],
        scratch_shapes=list(scratch),
        compiler_params=pltpu.CompilerParams(vmem_limit_bytes=mib << 20),
        cost_estimate=pl.CostEstimate(
            flops=flops, bytes_accessed=nbytes, transcendentals=0
        ),
    )

    def on_chip(*args):
        made = run(
            *(
                pltpu.with_memory_space_constraint(a, pltpu.VMEM) if s is VMEM else a
                for a, s in zip(args, specs)
            )
        )
        return [
            o if auto or n in in_hbm else pltpu.with_memory_space_constraint(o, pltpu.VMEM)
            for n, o in enumerate(made)
        ]

    return on_chip


def local(grad_out, gate_act, up_act, w_gate, w_up, w_down):
    tokens, d = grad_out.shape
    ff = gate_act.shape[1]
    share = tokens // (NX * NC)
    cols = d // NY
    width = cols // PIECES
    blk = tokens // NC // NX
    table = jnp.asarray(tables(tokens))
    gate_t, up_t = gate_act.T, up_act.T

    packed_rows = 2 * PIECES * share + tokens // 2 + tokens // 4
    dma = pltpu.SemaphoreType.DMA
    small = [
        pltpu.VMEM(table.shape, jnp.int32),
        pltpu.VMEM((ff, tokens), bf16),
        pltpu.VMEM((ff, tokens), bf16),
    ]
    head = d // CHUNKS * HEAD
    packed, part = call(
        pack_kernel,
        [HBM] * 5,
        [(NY, packed_rows, width), (ff, tokens)],
        tokens * ff * d,
        7_000_000,
        small
        + [
            pltpu.VMEM((2, share, d), bf16),
            pltpu.VMEM((NY, 2 * PIECES * share, width), bf16),
            pltpu.VMEM((packed_rows - 2 * PIECES * share, width), bf16),
            pltpu.VMEM((tokens, head), bf16),
            pltpu.VMEM((ff, head), bf16),
            dma((3,)),
            dma((2,)),
            dma((NY,)),
            dma((NY,)),
            dma((HEAD,)),
            dma((HEAD,)),
        ],
        in_hbm=(0,),
        mib=63,
        dtype=(bf16, f32),
    )(table, gate_t, up_t, grad_out, w_down)
    packed = lax.all_to_all(packed, "y", 0, 0)

    their_far, their_near, our_far, our_near = call(
        main_kernel,
        [VMEM] + [HBM] * 7,
        [(blk, d), (3 * blk, d), (blk, d), (3 * blk, d)],
        5 * tokens * ff * d,
        12_000_000,
        small
        + [
            pltpu.VMEM((tokens, d - head), bf16),
            pltpu.VMEM((ff, d - head), bf16),
            pltpu.VMEM((2 * ff, d), bf16),
            dma((3,)),
        ]
        + [dma((CHUNKS - HEAD,))] * 2
        + [dma((CHUNKS,))] * 2,
        mib=58,
    )(part, table, gate_t, up_t, grad_out, w_down, w_gate, w_up)
    their_far = lax.ppermute(their_far, "c", shift(NC, 1))
    their_near = lax.ppermute(their_near, "c", shift(NC, 1))
    (far,) = call(add_kernel, [VMEM] * 2, [(blk, d)], blk * d, 6 * blk * d)(
        our_far, their_far
    )
    far = lax.ppermute(far, ("x", "c"), round_x(1))
    own, via, other = call(
        near_kernel,
        [VMEM] * 2,
        [(blk, d)] * 3,
        3 * blk * d,
        22 * blk * d,
        dtype=(f32, f32, bf16),
    )(our_near, their_near)
    other = lax.ppermute(other, ("x", "c"), round_x(-1))
    (via,) = call(add_kernel, [VMEM] * 2, [(blk, d)], blk * d, 8 * blk * d)(via, far)
    via = lax.ppermute(via, ("x", "c"), round_x(1))
    (own,) = call(
        own_kernel, [VMEM] * 3, [(NZ, blk // NZ, d)], 2 * blk * d, 10 * blk * d
    )(own, via, other)
    parts = lax.all_to_all(own, "z", 0, 0)
    (input_grad,) = call(
        total_kernel, [VMEM], [(blk // NZ, d)], blk * d, 3 * blk * d, auto=True
    )(parts)

    mine = packed[:, : 2 * PIECES * share, :]
    side = lax.ppermute(mine, ("x", "c"), round_x(-1))
    core = lax.ppermute(mine, "c", shift(NC, 1))
    side_core = lax.ppermute(side, "c", shift(NC, 1))
    early, late = 6 * NY * share, 2 * NY * share
    (part,) = call(
        down_kernel,
        [VMEM] * 3,
        [(ff, cols)],
        2 * early * ff * cols,
        6_000_000,
        [pltpu.VMEM((early, ff), bf16), pltpu.VMEM((early, cols), bf16)],
        dtype=(f32,),
    )(packed, side, core)
    (down_grad,) = call(
        last_kernel,
        [VMEM] * 3,
        [(ff, cols)],
        2 * late * ff * cols,
        3_000_000,
        [pltpu.VMEM((late, ff), bf16), pltpu.VMEM((late, cols), bf16)],
        auto=True,
    )(packed, side_core, part)
    return (input_grad, down_grad)


def solution(mesh):
    mesh4 = Mesh(mesh.devices.reshape(NY, NZ, NX, NC), ("y",) + PLANE)
    placed = (
        P("y", None),
        P("y", PLANE),
        P("y", PLANE),
        P(PLANE, None),
        P(PLANE, None),
        P(PLANE, None),
    )
    return jax.shard_map(
        local,
        mesh=mesh4,
        in_specs=placed,
        out_specs=(P(("y",) + PLANE, None), P(PLANE, "y")),
        check_vma=False,
    )
```

```python
import jax
import jax.numpy as jnp
import numpy as np
from jax import lax
from jax.experimental import pallas as pl
from jax.experimental.pallas import tpu as pltpu
from jax.sharding import Mesh, PartitionSpec as P

NY, NZ, NX, NC = 8, 12, 4, 2
PLANE = ("z", "x", "c")
CHUNKS = 4
HEAD = 2
PIECES = 4
LANES = 128
f32, bf16 = jnp.float32, jnp.bfloat16


VMEM = pl.BlockSpec(memory_space=pltpu.VMEM)
HBM = pl.BlockSpec(memory_space=pltpu.HBM)


def shift(n, d):
    return [(i, (i + d) % n) for i in range(n)]


def round_x(step):
    return [
        (x * NC + c, (x + step * (1 - 2 * c)) % NX * NC + c)
        for x in range(NX)
        for c in range(NC)
    ]


def dot(a, b, over):
    return lax.dot_general(a, b, (over, ((), ())), preferred_element_type=f32)


def one_hot(order):
    n = order.shape[0]
    cols = lax.broadcasted_iota(jnp.int32, (n, n), 1)
    return jnp.where(cols == order, 1.0, 0.0).astype(bf16)


def tables(tokens):
    share = tokens // (NX * NC)
    per = share // NZ
    i = np.arange(tokens)
    j, k, rest = i // (NX * share), (i // share) % NX, i % share
    by_owner = (rest // per) * (NX * NC * per) + rest % per
    return np.stack([k, j, rest, by_owner], axis=1).astype(np.int32)


def rows_of(table, base, x_step, c_step):
    c = (lax.axis_index("c") + table[:, 1:2]) & (NC - 1)
    x = (lax.axis_index("x") + table[:, 0:1] * (1 - 2 * c)) & (NX - 1)
    return table[:, base : base + 1] + x * x_step + c * c_step


def load_chunks(grad_hbm, wd_hbm, grad, wd, grad_sem, wd_sem, first):
    step = grad_hbm.shape[1] // CHUNKS
    pairs = []
    for i in range(grad.shape[1] // step):
        here, there = pl.ds((first + i) * step, step), pl.ds(i * step, step)
        pairs.append(
            (
                pltpu.make_async_copy(
                    grad_hbm.at[:, here], grad.at[:, there], grad_sem.at[i]
                ),
                pltpu.make_async_copy(wd_hbm.at[:, here], wd.at[:, there], wd_sem.at[i]),
            )
        )
    return pairs


def contract(loads, grad, wd, behind=()):
    step = grad.shape[1] // len(loads)
    total = jnp.zeros((wd.shape[0], grad.shape[0]), f32)
    for i, pair in enumerate(loads):
        for copy in pair:
            copy.wait()
        for copy in behind[i * len(behind) // len(loads) :][: len(behind) // len(loads)]:
            copy.start()
        at = slice(i * step, (i + 1) * step)
        total = total + dot(wd[:, at], grad[:, at], ((1,), (1,)))
    return total


def pack_kernel(
    table_hbm, gate_hbm, up_hbm, grad_hbm, wd_hbm, packed_hbm, part_ref,
    table, gate_v, up_v, grad, mine, hid, gradc, wd,
    small_sem, grad_sem, mine_sem, hid_sem, gradc_sem, wd_sem,
):
    ff, tokens = gate_v.shape
    ny, mine_rows, width = mine.shape
    share = grad.shape[1]
    small = [
        pltpu.make_async_copy(a, b, small_sem.at[i])
        for i, (a, b) in enumerate(
            ((gate_hbm, gate_v), (up_hbm, up_v), (table_hbm, table))
        )
    ]
    x, c = lax.axis_index("x"), lax.axis_index("c")
    for n in range(2):
        first = (((x + 2 * n) & (NX - 1)) * NC + c) * share
        rows = pl.ds(pl.multiple_of(first, 8), share)
        small.append(
            pltpu.make_async_copy(grad_hbm.at[rows, :], grad.at[n], grad_sem.at[n])
        )
    loads = load_chunks(grad_hbm, wd_hbm, gradc, wd, gradc_sem, wd_sem, 0)
    for copy in small:
        copy.start()
    for pair in loads:
        for copy in pair:
            copy.start()
    for copy in small[:3]:
        copy.wait()
    gate = gate_v[...].astype(f32)
    hidden = (gate * jax.nn.sigmoid(gate) * up_v[...].astype(f32)).astype(bf16)
    order = rows_of(table[...], 2, NC * share, share)
    hidden = dot(one_hot(order), hidden, ((1,), (1,))).astype(bf16)
    half, quarter = tokens // 2, tokens // 4
    for n in range(2):
        lanes = slice(n * LANES, (n + 1) * LANES)
        hid[:half, lanes] = hidden[n * half : (n + 1) * half, :LANES]
    rest = jnp.zeros((quarter, LANES // 2 - (ff - LANES)), bf16)
    for n in range(2):
        lanes = slice(n * LANES, (n + 1) * LANES)
        groups = []
        for m in (2 * n, 2 * n + 1):
            groups += [hidden[m * quarter : (m + 1) * quarter, LANES:], rest]
        hid[half:, lanes] = jnp.concatenate(groups, axis=1)
    stores = [
        pltpu.make_async_copy(hid, packed_hbm.at[y, mine_rows:, :], hid_sem.at[y])
        for y in range(ny)
    ]
    for copy in stores:
        copy.start()
    for copy in small[3:]:
        copy.wait()
    for y in range(ny):
        for n in range(2):
            for b in range(PIECES):
                start = (y * PIECES + b) * width
                row = (n * PIECES + b) * share
                mine[y, row : row + share, :] = grad[n, :, start : start + width]
        copy = pltpu.make_async_copy(
            mine.at[y], packed_hbm.at[y, :mine_rows, :], mine_sem.at[y]
        )
        copy.start()
        stores.append(copy)
    part_ref[...] = contract(loads, gradc, wd)
    for copy in stores:
        copy.wait()


def main_kernel(
    part_ref, table_hbm, gate_hbm, up_hbm, grad_hbm, wd_hbm, wg_hbm, wu_hbm,
    their_far, their_near, our_far, our_near,
    table, gate_v, up_v, grad, wd, w, small_sem, grad_sem, wd_sem, wg_sem, wu_sem,
):
    d = w.shape[1]
    ff = wd.shape[0]
    blk = our_far.shape[0]
    step = d // CHUNKS
    chunks = [pl.ds(i * step, step) for i in range(CHUNKS)]
    small = [
        pltpu.make_async_copy(a, b, small_sem.at[i])
        for i, (a, b) in enumerate(
            ((gate_hbm, gate_v), (up_hbm, up_v), (table_hbm, table))
        )
    ]
    loads = load_chunks(grad_hbm, wd_hbm, grad, wd, grad_sem, wd_sem, HEAD)
    weights = [
        (
            pltpu.make_async_copy(wg_hbm.at[:, c], w.at[:ff, c], wg_sem.at[i]),
            pltpu.make_async_copy(wu_hbm.at[:, c], w.at[ff:, c], wu_sem.at[i]),
        )
        for i, c in enumerate(chunks)
    ]
    for copy in small:
        copy.start()
    for pair in loads:
        for copy in pair:
            copy.start()

    for copy in small:
        copy.wait()
    gate = gate_v[...].astype(f32)
    up = up_v[...].astype(f32)
    sig = jax.nn.sigmoid(gate)
    silu = gate * sig
    slope = up * sig * (1.0 + gate * (1.0 - sig))
    per = blk // NZ
    pick = one_hot(rows_of(table[...], 3, NC * per, per))
    behind = [copy for pair in weights for copy in pair]
    hidden_grad = part_ref[...] + contract(loads, grad, wd, behind)
    both = jnp.concatenate(
        [(hidden_grad * slope).astype(bf16), (hidden_grad * silu).astype(bf16)], axis=0
    )
    both = dot(pick, both, ((1,), (1,))).astype(bf16)
    for i, pair in enumerate(weights):
        for copy in pair:
            copy.wait()
        for n in range(step // 512):
            at = slice(i * step + n * 512, i * step + (n + 1) * 512)
            part = dot(both, w[:, at], ((1,), (0,))).astype(bf16)
            for far, near, first in (
                (our_far, our_near, 0),
                (their_far, their_near, NX),
            ):
                rows = [
                    part[(first + k) * blk : (first + k + 1) * blk] for k in range(NX)
                ]
                near[:blk, at] = rows[0]
                near[blk : 2 * blk, at] = rows[1]
                far[:, at] = rows[2]
                near[2 * blk :, at] = rows[3]


def add_kernel(a_ref, b_ref, out_ref):
    out_ref[...] = (a_ref[...].astype(f32) + b_ref[...].astype(f32)).astype(bf16)


def near_kernel(a_ref, b_ref, own_ref, via_ref, other_ref):
    blk = own_ref.shape[0]
    for n, ref in enumerate((own_ref, via_ref, other_ref)):
        rows = slice(n * blk, (n + 1) * blk)
        total = a_ref[rows].astype(f32) + b_ref[rows].astype(f32)
        ref[...] = total.astype(ref.dtype)


def own_kernel(own_ref, via_ref, other_ref, out_ref):
    nz, per, _ = out_ref.shape
    total = own_ref[...] + via_ref[...].astype(f32) + other_ref[...].astype(f32)
    for z in range(nz):
        out_ref[z] = total[z * per : (z + 1) * per].astype(bf16)


def total_kernel(parts_ref, out_ref):
    total = parts_ref[0].astype(f32)
    for z in range(1, parts_ref.shape[0]):
        total = total + parts_ref[z].astype(f32)
    out_ref[...] = total.astype(bf16)


def gather_rows(jks, piece_of, own_ref, h, g):
    ny, _, width = own_ref.shape
    block = h.shape[0] // len(jks)
    share = block // ny
    for n, jk in enumerate(jks):
        rows = slice(n * block, (n + 1) * block)
        first = 2 * PIECES * share
        at, lane = first + jk % 4 * share, jk // 4 * LANES
        h[rows, :LANES] = own_ref[:, at : at + share, lane : lane + LANES].reshape(
            block, LANES
        )
        at, lane = first + (4 + jk % 2) * share, jk // 2 * (LANES // 2)
        h[rows, LANES:] = own_ref[
            :, at : at + share, lane : lane + h.shape[1] - LANES
        ].reshape(block, h.shape[1] - LANES)
        for b in range(PIECES):
            piece = piece_of(jk, b, share)
            g[rows, b * width : (b + 1) * width] = piece.reshape(block, width)


def down_kernel(own_ref, side_ref, side2_ref, core_ref, next_ref, out_ref, h, g):
    def piece_of(jk, b, share):
        first = b * share
        if jk % 2 == 0:
            first = (jk % NX // 2 * PIECES + b) * share
            ref = own_ref if jk < NX else core_ref
        elif jk < NX:
            ref = side_ref if jk == 1 else side2_ref
        else:
            ref = next_ref
        return ref[:, first : first + share, :]

    gather_rows((0, 1, 2, 3, NX, NX + 1, NX + 2), piece_of, own_ref, h, g)
    left = h[...]
    width = own_ref.shape[2]
    for b in range(PIECES):
        c = slice(b * width, (b + 1) * width)
        out_ref[:, c] = dot(left, g[:, c], ((0,), (0,)))


def last_kernel(own_ref, side_ref, sum_ref, out_ref, h, g):
    def piece_of(jk, b, share):
        return side_ref[:, b * share : (b + 1) * share, :]

    gather_rows((NX + 3,), piece_of, own_ref, h, g)
    left = h[...]
    width = own_ref.shape[2]
    for b in range(PIECES):
        c = slice(b * width, (b + 1) * width)
        part = dot(left, g[:, c], ((0,), (0,)))
        out_ref[:, c] = (sum_ref[:, c] + part).astype(bf16)


def call(kernel, specs, outs, flops, nbytes, scratch=(), in_hbm=(), auto=False, mib=16, dtype=None):
    dtypes = dtype or (bf16,) * len(outs)
    run = pl.pallas_call(
        kernel,
        in_specs=specs,
        out_specs=[HBM if n in in_hbm else VMEM for n in range(len(outs))],
        out_shape=[
            jax.ShapeDtypeStruct(s, t) if auto or n in in_hbm else pltpu.VMEM(s, t)
            for n, (s, t) in enumerate(zip(outs, dtypes))
        ],
        scratch_shapes=list(scratch),
        compiler_params=pltpu.CompilerParams(vmem_limit_bytes=mib << 20),
        cost_estimate=pl.CostEstimate(
            flops=flops, bytes_accessed=nbytes, transcendentals=0
        ),
    )

    def on_chip(*args):
        made = run(
            *(
                pltpu.with_memory_space_constraint(a, pltpu.VMEM) if s is VMEM else a
                for a, s in zip(args, specs)
            )
        )
        return [
            o if auto or n in in_hbm else pltpu.with_memory_space_constraint(o, pltpu.VMEM)
            for n, o in enumerate(made)
        ]

    return on_chip


def local(grad_out, gate_act, up_act, w_gate, w_up, w_down):
    tokens, d = grad_out.shape
    ff = gate_act.shape[1]
    share = tokens // (NX * NC)
    cols = d // NY
    width = cols // PIECES
    blk = tokens // NC // NX
    table = jnp.asarray(tables(tokens))
    gate_t, up_t = gate_act.T, up_act.T

    packed_rows = 2 * PIECES * share + tokens // 2 + tokens // 4
    dma = pltpu.SemaphoreType.DMA
    small = [
        pltpu.VMEM(table.shape, jnp.int32),
        pltpu.VMEM((ff, tokens), bf16),
        pltpu.VMEM((ff, tokens), bf16),
    ]
    head = d // CHUNKS * HEAD
    packed, part = call(
        pack_kernel,
        [HBM] * 5,
        [(NY, packed_rows, width), (ff, tokens)],
        tokens * ff * d,
        7_000_000,
        small
        + [
            pltpu.VMEM((2, share, d), bf16),
            pltpu.VMEM((NY, 2 * PIECES * share, width), bf16),
            pltpu.VMEM((packed_rows - 2 * PIECES * share, width), bf16),
            pltpu.VMEM((tokens, head), bf16),
            pltpu.VMEM((ff, head), bf16),
            dma((3,)),
            dma((2,)),
            dma((NY,)),
            dma((NY,)),
            dma((HEAD,)),
            dma((HEAD,)),
        ],
        in_hbm=(0,),
        mib=63,
        dtype=(bf16, f32),
    )(table, gate_t, up_t, grad_out, w_down)
    packed = lax.all_to_all(packed, "y", 0, 0)

    their_far, their_near, our_far, our_near = call(
        main_kernel,
        [VMEM] + [HBM] * 7,
        [(blk, d), (3 * blk, d), (blk, d), (3 * blk, d)],
        5 * tokens * ff * d,
        12_000_000,
        small
        + [
            pltpu.VMEM((tokens, d - head), bf16),
            pltpu.VMEM((ff, d - head), bf16),
            pltpu.VMEM((2 * ff, d), bf16),
            dma((3,)),
        ]
        + [dma((CHUNKS - HEAD,))] * 2
        + [dma((CHUNKS,))] * 2,
        mib=58,
    )(part, table, gate_t, up_t, grad_out, w_down, w_gate, w_up)
    their_far = lax.ppermute(their_far, "c", shift(NC, 1))
    their_near = lax.ppermute(their_near, "c", shift(NC, 1))
    (far,) = call(add_kernel, [VMEM] * 2, [(blk, d)], blk * d, 6 * blk * d)(
        our_far, their_far
    )
    far = lax.ppermute(far, ("x", "c"), round_x(1))
    own, via, other = call(
        near_kernel,
        [VMEM] * 2,
        [(blk, d)] * 3,
        3 * blk * d,
        22 * blk * d,
        dtype=(f32, f32, bf16),
    )(our_near, their_near)
    other = lax.ppermute(other, ("x", "c"), round_x(-1))
    (via,) = call(add_kernel, [VMEM] * 2, [(blk, d)], blk * d, 8 * blk * d)(via, far)
    via = lax.ppermute(via, ("x", "c"), round_x(1))
    (own,) = call(
        own_kernel, [VMEM] * 3, [(NZ, blk // NZ, d)], 2 * blk * d, 10 * blk * d
    )(own, via, other)
    parts = lax.all_to_all(own, "z", 0, 0)
    (input_grad,) = call(
        total_kernel, [VMEM], [(blk // NZ, d)], blk * d, 3 * blk * d, auto=True
    )(parts)

    mine = packed[:, : 2 * PIECES * share, :]
    part_rows = PIECES * share
    side = lax.ppermute(mine[:, :part_rows], ("x", "c"), round_x(-1))
    side2 = lax.ppermute(mine[:, part_rows:], ("x", "c"), round_x(-1))
    core = lax.ppermute(mine, "c", shift(NC, 1))
    side_core = lax.ppermute(side, "c", shift(NC, 1))
    side_core2 = lax.ppermute(side2, "c", shift(NC, 1))
    early, late = 7 * NY * share, NY * share
    (part,) = call(
        down_kernel,
        [VMEM] * 5,
        [(ff, cols)],
        2 * early * ff * cols,
        6_000_000,
        [pltpu.VMEM((early, ff), bf16), pltpu.VMEM((early, cols), bf16)],
        dtype=(f32,),
    )(packed, side, side2, core, side_core)
    (down_grad,) = call(
        last_kernel,
        [VMEM] * 3,
        [(ff, cols)],
        2 * late * ff * cols,
        3_000_000,
        [pltpu.VMEM((late, ff), bf16), pltpu.VMEM((late, cols), bf16)],
        auto=True,
    )(packed, side_core2, part)
    return (input_grad, down_grad)


def solution(mesh):
    mesh4 = Mesh(mesh.devices.reshape(NY, NZ, NX, NC), ("y",) + PLANE)
    placed = (
        P("y", None),
        P("y", PLANE),
        P("y", PLANE),
        P(PLANE, None),
        P(PLANE, None),
        P(PLANE, None),
    )
    return jax.shard_map(
        local,
        mesh=mesh4,
        in_specs=placed,
        out_specs=(P(("y",) + PLANE, None), P(PLANE, "y")),
        check_vma=False,
    )
```
